32 devices in a mesh: sub: 8 (over z, y), grp: 4 (over x, core).
Axes of the slice: x: 2, y: 2, z: 4, core: 2. Of those that a mesh axis runs over, the one named last changes fastest.
Arguments:
- interior_factor: bfloat16 [32, 2048, 2048], P(('sub', 'grp')), may hold values from -0.25 to 2, as said below
- interface_coupling: bfloat16 [32, 2048, 512], P(('sub', 'grp')), may hold values from -0.09375 to 0.09375
- interface_block: float32 [32, 512, 512], P(('sub', 'grp')), may hold values from -0.5 to 4, as said below
- sample_panel: bfloat16 [4096, 128], P('sub'), may hold values from -6 to 6
- index_map: int32 [32, 4], P(('sub', 'grp')), may hold values from 0 to 31, as said below
- block_count: int32 [32], P(('sub', 'grp')), may hold values from 1 to 4
Outputs:
- sampled: float32 [4096, 128], P(('sub', 'grp'))
The draws below stay inside these ranges and needn't reach their ends.
Inputs may be any that keep to these rules, and one draw needn't show every extreme that they name: `index_map`: local block a of subdomain s is global block o * 4 + a, where o is s // 4, or one more or one less than it modulo 32 // 4. `interior_factor`: each matrix is lower triangular with its diagonal in 1 to 2. `interface_block`: each matrix is symmetric with its diagonal in 2 to 4.
All inputs are finite; a program needn't handle non-finite values.
Results may differ from the reference program's by a relative error of at most 0.0012.
Values sent between devices are 32-bit elements; how exact they have to be, the bound alone decides.
No kernel may reach another device: no remote copies, remote signals or barrier semaphores. Data moves between devices by JAX's collectives and lax.ppermute only.
A program may use at most 64 MiB of HBM per device.

```python
import jax
import jax.numpy as jnp
from jax import lax

NI = 2048
NB = 512
BLK = 128
NS = 128
POWER = 3
LB = 4
NSUBD = 32
NG = 4096


def draw_interior_factor(key, part):

    def one_factor(sub_key):
        first, second = jax.random.split(sub_key)
        diagonal = jax.random.uniform(first, (NI,), jnp.float32, 1.0, 2.0)
        lower = jax.random.normal(second, (NI, NI), jnp.float32) * NI ** (-0.5)
        lower = jnp.clip(lower, -0.25, 0.25)
        matrix = jnp.tril(lower, -1) + jnp.diag(diagonal)
        return matrix.astype(jnp.bfloat16)
    return lax.map(one_factor, jax.random.split(key, NSUBD))


def draw_interface_block(key, part):

    def one_block(sub_key):
        first, second = jax.random.split(sub_key)
        diagonal = jax.random.uniform(first, (NB,), jnp.float32, 2.0, 4.0)
        noise = jax.random.normal(second, (NB, NB), jnp.float32) * 0.05
        symmetric = (noise + noise.T) * 0.7071
        symmetric = symmetric - jnp.diag(jnp.diag(symmetric))
        return symmetric + jnp.diag(diagonal)
    return lax.map(one_block, jax.random.split(key, NSUBD))


def draw_index_map(key, part):
    offsets = jax.random.randint(jax.random.fold_in(key, 7), (NSUBD, LB), -1, 2)
    cycles = NSUBD // LB
    home = jnp.arange(NSUBD, dtype=jnp.int32) // LB
    owner = (home[:, None] + offsets + cycles) % cycles
    return (owner * LB + jnp.arange(LB, dtype=jnp.int32)[None, :]).astype(jnp.int32)


def touch_ends(result, stream_key, least, top_value):
    spot = [jax.random.randint(jax.random.fold_in(stream_key, axis), (), 0, length) for axis, length in enumerate(result.shape)]
    longest = result.shape.index(max(result.shape))
    beside = spot[:longest] + [(spot[longest] + 1) % result.shape[longest]] + spot[longest + 1:]
    return result.at[tuple(spot)].set(least).at[tuple(beside)].set(top_value)


def level_of(stream_key, shape, cuts, low, largest):
    level, own = 1.0, jax.random.fold_in(stream_key, 6)
    for position, parts in cuts:
        heights = jnp.exp(jax.random.uniform(jax.random.fold_in(own, position), (parts,), jnp.float32, low / len(cuts), largest / len(cuts)))
        level = level * jnp.repeat(heights, shape[position] // parts).reshape([-1 if axis == position else 1 for axis in range(len(shape))])
    return level


def centred(rng, dims, deviation, limit, cuts=(), held_as=jnp.bfloat16):
    values = jax.random.normal(rng, dims, jnp.float32) * deviation
    if len(cuts) > 0:
        values = level_of(rng, dims, cuts, -0.22, 0.18) * values
    return jnp.clip(values, min=-limit, max=limit).astype(held_as)


def setup_inputs(seed: int = 0) -> dict:
    key_of = jax.random.split(jax.random.key(seed), 7)
    return {
        "interior_factor": draw_interior_factor(jax.random.fold_in(key_of[6], 71), 0),
        "interface_coupling": centred(key_of[1], (NSUBD, NI, NB), (2 * NI) ** -0.5, 0.09375, ((0, 32),)),
        "interface_block": draw_interface_block(jax.random.fold_in(key_of[6], 71), 0),
        "sample_panel": centred(key_of[3], (NG, NS), 1.0, 6.0, ((0, 8),)),
        "index_map": draw_index_map(jax.random.fold_in(key_of[6], 71), 0),
        "block_count": touch_ends(jax.random.randint(key_of[5], (NSUBD,), 1, LB + 1), jax.random.fold_in(key_of[5], 1), 1, LB).astype(jnp.int32),
    }


def form_schur(items):
    factor, coupling, block, count = items
    coupled = jnp.dot(factor, coupling, preferred_element_type=jnp.float32).astype(jnp.bfloat16)
    schur = block - jnp.dot(coupled.T, coupled, preferred_element_type=jnp.float32)
    live = (jnp.arange(LB, dtype=jnp.int32) < count).astype(jnp.float32)
    masked = schur.reshape(LB, BLK, LB, BLK) * live[:, None, None, None] * live[None, None, :, None]
    return masked.reshape(NB, NB)


def apply_fn(vector_blocks):
    def apply_one(items):
        masked, ids = items
        picked = vector_blocks[ids]
        product = jnp.dot(masked, picked.reshape(NB, NS), precision=lax.Precision.HIGHEST)
        return product.reshape(LB, BLK, NS)
    return apply_one


def reference(interior_factor, interface_coupling, interface_block, sample_panel, index_map, block_count):
    schurs = lax.map(form_schur, (interior_factor, interface_coupling, interface_block, block_count))
    vector_blocks = sample_panel.astype(jnp.float32).reshape(NSUBD, BLK, NS)
    for step in range(POWER):
        terms = lax.map(apply_fn(vector_blocks), (schurs, index_map))
        total = jnp.zeros((NSUBD, BLK, NS), jnp.float32)
        total = total.at[index_map.reshape(-1)].add(terms.reshape(NSUBD * LB, BLK, NS))
        vector_blocks = 0.5 * total
    return vector_blocks.reshape(NG, NS)
```

```python
import jax
import jax.numpy as jnp
from jax import lax
from jax.experimental import pallas as pl
from jax.experimental.pallas import tpu as pltpu
from jax.sharding import PartitionSpec as P

POWER = 3
TILE = 256
TAIL = 8


def sub_shift(block, distance):
    size = lax.axis_size("sub")
    return lax.ppermute(block, "sub", [(i, (i + distance) % size) for i in range(size)])


def grp_shift(block, distance):
    size = lax.axis_size("grp")
    return lax.ppermute(block, "grp", [(i, (i + distance) % size) for i in range(size)])


def schur_kernel(info, factor, coupling, block, high, low, fbuf, cbuf, bbuf, coupled, fsem, csem, bsem):
    ni, width = coupling.shape
    nblk = info.shape[0] - 2
    blk = width // nblk
    steps = ni // TILE
    rows = [pl.ds(i * TILE, TILE) for i in range(steps)]
    loads = []
    for i in range(steps):
        ccopy = pltpu.make_async_copy(coupling.at[rows[i]], cbuf.at[rows[i]], csem.at[i])
        span = pl.ds(0, (i + 1) * TILE)
        fcopy = pltpu.make_async_copy(factor.at[rows[i], span], fbuf.at[rows[i], span], fsem.at[i])
        ccopy.start()
        fcopy.start()
        loads.append((ccopy, fcopy))
    bcopy = pltpu.make_async_copy(block, bbuf, bsem)
    bcopy.start()
    for i in range(steps):
        for copy in loads[i]:
            copy.wait()
        span = (i + 1) * TILE
        part = jnp.dot(
            fbuf[rows[i], 0:span], cbuf[0:span, :], preferred_element_type=jnp.float32
        )
        coupled[rows[i], :] = part.astype(jnp.bfloat16)
    gram = lax.dot_general(
        coupled[...], coupled[...], (((0,), (0,)), ((), ())), preferred_element_type=jnp.float32
    )
    bcopy.wait()
    member = info[0]
    count = info[1]
    for a in range(nblk):
        row = pl.multiple_of(lax.rem(a - member + nblk, nblk) * blk, blk)
        for b in range(nblk):
            col = pl.multiple_of(lax.rem(member - b + nblk, nblk) * blk, blk)
            cut = (slice(a * blk, (a + 1) * blk), slice(b * blk, (b + 1) * blk))
            scale = jnp.where(max(a, b) < count, 0.5, 0.0).astype(jnp.float32)
            value = (bbuf[cut] - gram[cut]) * scale
            top = value.astype(jnp.bfloat16)
            high[pl.ds(row, blk), pl.ds(col, blk)] = top
            low[pl.ds(row, blk), pl.ds(col, blk)] = (value - top.astype(jnp.float32)).astype(
                jnp.bfloat16
            )


def first_kernel(info, high, low, own, near, far, *terms):
    nblk = len(terms)
    blk = own.shape[0] // nblk
    member = info[0]
    even = lax.rem(member, 2) == 0
    picked = []
    for r in range(nblk):
        b = lax.rem(member - r + nblk, nblk)
        span = pl.ds(pl.multiple_of(b * blk, blk), blk)
        dest = info[2 + b]
        use_near = jnp.logical_or(
            jnp.logical_and(dest == -1, even), jnp.logical_and(dest == 1, jnp.logical_not(even))
        )
        other = jnp.where(use_near, near[span, :], far[span, :])
        picked.append(jnp.where(dest == 0, own[span, :], other))
    vector = jnp.concatenate(picked, axis=0).astype(jnp.bfloat16)
    product = jnp.dot(high[...], vector, preferred_element_type=jnp.float32)
    product = product + jnp.dot(low[...], vector, preferred_element_type=jnp.float32)
    for r in range(nblk):
        terms[r][0:blk, :] = product[r * blk : (r + 1) * blk, :]
        dest = info[2 + lax.rem(member + r, nblk)]
        terms[r][blk : blk + TAIL, :] = jnp.full(
            (TAIL, own.shape[1]), dest.astype(jnp.float32), jnp.float32
        )


def apply_kernel(high, low, *refs):
    nblk = len(refs) // 2
    blk = refs[0].shape[0]
    vector = jnp.concatenate([ref[...] for ref in refs[:nblk]], axis=0)
    top = vector.astype(jnp.bfloat16)
    rest = (vector - top.astype(jnp.float32)).astype(jnp.bfloat16)
    product = jnp.dot(high[...], top, preferred_element_type=jnp.float32)
    product = product + jnp.dot(high[...], rest, preferred_element_type=jnp.float32)
    product = product + jnp.dot(low[...], top, preferred_element_type=jnp.float32)
    for r in range(nblk):
        refs[nblk + r][...] = product[r * blk : (r + 1) * blk, :]


def local(
    interior_factor, interface_coupling, interface_block, sample_panel, index_map, block_count
):
    factor = interior_factor[0]
    coupling = interface_coupling[0]
    block = interface_block[0]
    ids = index_map[0]
    nblk = ids.shape[0]
    ni, width = coupling.shape
    blk = width // nblk
    samples = sample_panel.shape[1]
    cycles = lax.axis_size("sub")
    groups = lax.axis_size("grp")
    home = lax.axis_index("sub")
    member = lax.axis_index("grp").astype(jnp.int32)
    dest = (ids // groups - home + cycles + 1) % cycles - 1
    info = jnp.concatenate([member[None], block_count, dest]).astype(jnp.int32)
    smem = pl.BlockSpec(memory_space=pltpu.SMEM)
    anywhere = pl.BlockSpec(memory_space=pl.ANY)
    vmem = pl.BlockSpec(memory_space=pltpu.VMEM)

    own = sample_panel.astype(jnp.float32)
    route = []
    for o in range(cycles):
        for g in range(groups):
            step = 1 if g % 2 == 0 else -1
            route.append((o * groups + g, ((o + step) % cycles) * groups + g))
    near = lax.ppermute(own, ("sub", "grp"), route)

    steps = ni // TILE
    half = jax.ShapeDtypeStruct((width, width), jnp.bfloat16)
    high, low = pl.pallas_call(
        schur_kernel,
        out_shape=(half, half),
        in_specs=[smem, anywhere, anywhere, anywhere],
        out_specs=(vmem, vmem),
        scratch_shapes=[
            pltpu.VMEM((ni, ni), jnp.bfloat16),
            pltpu.VMEM((ni, width), jnp.bfloat16),
            pltpu.VMEM((width, width), jnp.float32),
            pltpu.VMEM((ni, width), jnp.bfloat16),
            pltpu.SemaphoreType.DMA((steps,)),
            pltpu.SemaphoreType.DMA((steps,)),
            pltpu.SemaphoreType.DMA,
        ],
        cost_estimate=pl.CostEstimate(
            flops=ni * ni * width + 2 * ni * width * width,
            bytes_accessed=ni * ni + 2 * ni * width + 4 * width * width,
            transcendentals=0,
        ),
        compiler_params=pltpu.CompilerParams(vmem_limit_bytes=32 * 1024 * 1024),
        name="schur",
    )(info, factor, coupling, block)

    far = lax.ppermute(near, "grp", [(g, g ^ 1) for g in range(groups)])
    tall = jax.ShapeDtypeStruct((blk + TAIL, samples), jnp.float32)
    short = jax.ShapeDtypeStruct((blk, samples), jnp.float32)
    terms = pl.pallas_call(
        first_kernel,
        out_shape=(tall,) * nblk,
        in_specs=[smem] + [vmem] * 5,
        out_specs=(vmem,) * nblk,
        name="first",
    )(info, high, low, own, near, far)

    owners = None
    for step in range(POWER):
        if step > 0:
            terms = pl.pallas_call(
                apply_kernel,
                out_shape=(short,) * nblk,
                in_specs=[vmem] * (2 + nblk),
                out_specs=(vmem,) * nblk,
                name="apply",
            )(high, low, *picked)
        got = [terms[0]] + [grp_shift(terms[r], r) for r in range(1, groups)]
        if step == 0:
            owners = [g[blk : blk + 1, :] for g in got]
            got = [g[:blk] for g in got]
        zero = jnp.zeros((blk, samples), jnp.float32)
        sums = {}
        for d in (-1, 0, 1):
            sums[d] = sum(jnp.where(owners[r] == d, got[r], zero) for r in range(groups))
        if step + 1 < POWER:
            behind = sub_shift(jnp.concatenate([sums[0], sums[1]]), 1)
            ahead = sub_shift(jnp.concatenate([sums[0], sums[-1]]), -1)
            behind2 = sub_shift(sums[1], 2)
            ahead2 = sub_shift(sums[-1], -2)
            here = sums[0] + behind[blk:] + ahead[blk:]
            after = ahead[:blk] + sums[1] + ahead2
            before = behind[:blk] + sums[-1] + behind2
            picked = []
            for r in range(groups):
                owner = owners[(groups - r) % groups]
                chosen = jnp.where(owner == 0, here, jnp.where(owner == 1, after, before))
                picked.append(chosen if r == 0 else grp_shift(chosen, r))
    return sums[0] + sub_shift(sums[1], 1) + sub_shift(sums[-1], -1)


def solution(mesh):
    return jax.shard_map(
        local,
        mesh=mesh,
        in_specs=(
            P(("sub", "grp"), None, None),
            P(("sub", "grp"), None, None),
            P(("sub", "grp"), None, None),
            P("sub", None),
            P(("sub", "grp"), None),
            P(("sub", "grp")),
        ),
        out_specs=P(("sub", "grp"), None),
        check_vma=False,
    )
```

```python
import jax
import jax.numpy as jnp
from jax import lax
from jax.experimental import pallas as pl
from jax.experimental.pallas import tpu as pltpu
from jax.sharding import PartitionSpec as P

POWER = 3
TILE = 256
TAIL = 8


def sub_shift(block, distance):
    size = lax.axis_size("sub")
    return lax.ppermute(block, "sub", [(i, (i + distance) % size) for i in range(size)])


def grp_shift(block, distance):
    size = lax.axis_size("grp")
    return lax.ppermute(block, "grp", [(i, (i + distance) % size) for i in range(size)])


def offset_of(ids, b):
    cycles = lax.axis_size("sub")
    owner = ids[0, b] // lax.axis_size("grp")
    return lax.rem(owner - lax.axis_index("sub") + cycles + 1, cycles) - 1


def schur_kernel(live, factor, coupling, block, high, low, fbuf, cbuf, bbuf, coupled, fsem, csem, bsem):
    ni, width = coupling.shape
    nblk = lax.axis_size("grp")
    blk = width // nblk
    steps = ni // TILE
    rows = [pl.ds(i * TILE, TILE) for i in range(steps)]
    loads = []
    for i in range(steps):
        ccopy = pltpu.make_async_copy(coupling.at[rows[i]], cbuf.at[rows[i]], csem.at[i])
        span = pl.ds(0, (i + 1) * TILE)
        fcopy = pltpu.make_async_copy(factor.at[rows[i], span], fbuf.at[rows[i], span], fsem.at[i])
        ccopy.start()
        fcopy.start()
        loads.append((ccopy, fcopy))
    bcopy = pltpu.make_async_copy(block, bbuf, bsem)
    bcopy.start()
    for i in range(steps):
        for copy in loads[i]:
            copy.wait()
        span = (i + 1) * TILE
        part = jnp.dot(
            fbuf[rows[i], 0:span], cbuf[0:span, :], preferred_element_type=jnp.float32
        )
        coupled[rows[i], :] = part.astype(jnp.bfloat16)
    gram = lax.dot_general(
        coupled[...], coupled[...], (((0,), (0,)), ((), ())), preferred_element_type=jnp.float32
    )
    bcopy.wait()
    member = lax.axis_index("grp")
    count = live[0]
    for a in range(nblk):
        row = pl.multiple_of(lax.rem(a - member + nblk, nblk) * blk, blk)
        for b in range(nblk):
            col = pl.multiple_of(lax.rem(member - b + nblk, nblk) * blk, blk)
            cut = (slice(a * blk, (a + 1) * blk), slice(b * blk, (b + 1) * blk))
            scale = jnp.where(max(a, b) < count, 0.5, 0.0).astype(jnp.float32)
            value = (bbuf[cut] - gram[cut]) * scale
            top = value.astype(jnp.bfloat16)
            high[pl.ds(row, blk), pl.ds(col, blk)] = top
            low[pl.ds(row, blk), pl.ds(col, blk)] = (value - top.astype(jnp.float32)).astype(
                jnp.bfloat16
            )


def first_kernel(ids, high, low, own, near, far, *terms):
    nblk = len(terms)
    blk = own.shape[0] // nblk
    member = lax.axis_index("grp")
    even = lax.rem(member, 2) == 0
    picked = []
    for r in range(nblk):
        b = lax.rem(member - r + nblk, nblk)
        span = pl.ds(pl.multiple_of(b * blk, blk), blk)
        dest = offset_of(ids, b)
        use_near = jnp.logical_or(
            jnp.logical_and(dest == -1, even), jnp.logical_and(dest == 1, jnp.logical_not(even))
        )
        other = jnp.where(use_near, near[span, :], far[span, :])
        picked.append(jnp.where(dest == 0, own[span, :], other))
    vector = jnp.concatenate(picked, axis=0).astype(jnp.bfloat16)
    product = jnp.dot(high[...], vector, preferred_element_type=jnp.float32)
    product = product + jnp.dot(low[...], vector, preferred_element_type=jnp.float32)
    for r in range(nblk):
        terms[r][0:blk, :] = product[r * blk : (r + 1) * blk, :]
        dest = offset_of(ids, lax.rem(member + r, nblk))
        terms[r][blk : blk + TAIL, :] = jnp.full(
            (TAIL, own.shape[1]), dest.astype(jnp.float32), jnp.float32
        )


def apply_kernel(high, low, *refs):
    nblk = len(refs) // 2
    blk = refs[0].shape[0]
    vector = jnp.concatenate([ref[...] for ref in refs[:nblk]], axis=0)
    top = vector.astype(jnp.bfloat16)
    rest = (vector - top.astype(jnp.float32)).astype(jnp.bfloat16)
    product = jnp.dot(high[...], top, preferred_element_type=jnp.float32)
    product = product + jnp.dot(high[...], rest, preferred_element_type=jnp.float32)
    product = product + jnp.dot(low[...], top, preferred_element_type=jnp.float32)
    for r in range(nblk):
        refs[nblk + r][...] = product[r * blk : (r + 1) * blk, :]


def local(
    interior_factor, interface_coupling, interface_block, sample_panel, index_map, block_count
):
    factor = interior_factor[0]
    coupling = interface_coupling[0]
    block = interface_block[0]
    nblk = index_map.shape[1]
    ni, width = coupling.shape
    blk = width // nblk
    samples = sample_panel.shape[1]
    cycles = lax.axis_size("sub")
    groups = lax.axis_size("grp")
    assert nblk == groups
    smem = pl.BlockSpec(memory_space=pltpu.SMEM)
    anywhere = pl.BlockSpec(memory_space=pltpu.HBM)
    vmem = pl.BlockSpec(memory_space=pltpu.VMEM)

    small = pltpu.CompilerParams(vmem_limit_bytes=8 * 1024 * 1024)
    own = sample_panel.astype(jnp.float32)
    route = []
    for o in range(cycles):
        for g in range(groups):
            step = 1 if g % 2 == 0 else -1
            route.append((o * groups + g, ((o + step) % cycles) * groups + g))
    near = lax.ppermute(own, ("sub", "grp"), route)

    steps = ni // TILE
    half = jax.ShapeDtypeStruct((width, width), jnp.bfloat16)
    high, low = pl.pallas_call(
        schur_kernel,
        out_shape=(half, half),
        in_specs=[smem, anywhere, anywhere, anywhere],
        out_specs=(vmem, vmem),
        scratch_shapes=[
            pltpu.VMEM((ni, ni), jnp.bfloat16),
            pltpu.VMEM((ni, width), jnp.bfloat16),
            pltpu.VMEM((width, width), jnp.float32),
            pltpu.VMEM((ni, width), jnp.bfloat16),
            pltpu.SemaphoreType.DMA((steps,)),
            pltpu.SemaphoreType.DMA((steps,)),
            pltpu.SemaphoreType.DMA,
        ],
        cost_estimate=pl.CostEstimate(
            flops=ni * ni * width + 2 * ni * width * width,
            bytes_accessed=ni * ni + 2 * ni * width + 4 * width * width,
            transcendentals=0,
        ),
        compiler_params=pltpu.CompilerParams(vmem_limit_bytes=52 * 1024 * 1024),
        name="schur",
    )(block_count, factor, coupling, block)

    near, high = lax.optimization_barrier((near, high))
    far = lax.ppermute(near, "grp", [(g, g ^ 1) for g in range(groups)])
    tall = jax.ShapeDtypeStruct((blk + TAIL, samples), jnp.float32)
    short = jax.ShapeDtypeStruct((blk, samples), jnp.float32)
    terms = pl.pallas_call(
        first_kernel,
        out_shape=(tall,) * nblk,
        in_specs=[smem] + [vmem] * 5,
        out_specs=(vmem,) * nblk,
        compiler_params=small,
        name="first",
    )(index_map, high, low, own, near, far)

    owners = None
    for step in range(POWER):
        if step > 0:
            terms = pl.pallas_call(
                apply_kernel,
                out_shape=(short,) * nblk,
                in_specs=[vmem] * (2 + nblk),
                out_specs=(vmem,) * nblk,
                compiler_params=small,
                name="apply",
            )(high, low, *picked)
        got = [terms[0]] + [grp_shift(terms[r], r) for r in range(1, groups)]
        if step == 0:
            owners = [g[blk : blk + 1, :] for g in got]
            got = [g[:blk] for g in got]
        zero = jnp.zeros((blk, samples), jnp.float32)
        sums = {}
        for d in (-1, 0, 1):
            sums[d] = sum(jnp.where(owners[r] == d, got[r], zero) for r in range(groups))
        if step + 1 < POWER:
            behind = sub_shift(jnp.concatenate([sums[0], sums[1]]), 1)
            ahead = sub_shift(jnp.concatenate([sums[0], sums[-1]]), -1)
            behind2 = sub_shift(sums[1], 2)
            ahead2 = sub_shift(sums[-1], -2)
            here = sums[0] + behind[blk:] + ahead[blk:]
            after = ahead[:blk] + sums[1] + ahead2
            before = behind[:blk] + sums[-1] + behind2
            picked = []
            for r in range(groups):
                owner = owners[(groups - r) % groups]
                chosen = jnp.where(owner == 0, here, jnp.where(owner == 1, after, before))
                picked.append(chosen if r == 0 else grp_shift(chosen, r))
    return sums[0] + sub_shift(sums[1], 1) + sub_shift(sums[-1], -1)


def solution(mesh):
    return jax.shard_map(
        local,
        mesh=mesh,
        in_specs=(
            P(("sub", "grp"), None, None),
            P(("sub", "grp"), None, None),
            P(("sub", "grp"), None, None),
            P("sub", None),
            P(("sub", "grp"), None),
            P(("sub", "grp")),
        ),
        out_specs=P(("sub", "grp"), None),
        check_vma=False,
    )
```

```python
import jax
import jax.numpy as jnp
from jax import lax
from jax.experimental import pallas as pl
from jax.experimental.pallas import tpu as pltpu
from jax.sharding import PartitionSpec as P

POWER = 3
TILE = 256
TAIL = 8


def sub_shift(block, distance):
    size = lax.axis_size("sub")
    return lax.ppermute(block, "sub", [(i, (i + distance) % size) for i in range(size)])


def grp_shift(block, distance):
    size = lax.axis_size("grp")
    return lax.ppermute(block, "grp", [(i, (i + distance) % size) for i in range(size)])


def offset_of(ids, b):
    cycles = lax.axis_size("sub")
    owner = ids[0, b] // lax.axis_size("grp")
    return lax.rem(owner - lax.axis_index("sub") + cycles + 1, cycles) - 1


def cross_shift(forward, backward, distance, even):
    size = lax.axis_size("sub")
    groups = lax.axis_size("grp")
    got = []
    for sign in (1, -1):
        route = []
        for o in range(size):
            for g in range(groups):
                step = sign * distance * (1 if g % 2 == 0 else -1)
                route.append((o * groups + g, ((o + step) % size) * groups + g))
        first, second = (forward, backward) if sign == 1 else (backward, forward)
        got.append(lax.ppermute(jnp.where(even, first, second), ("sub", "grp"), route))
    return jnp.where(even, got[0], got[1]), jnp.where(even, got[1], got[0])


def schur_kernel(live, factor, coupling, block, high, low, fbuf, cbuf, bbuf, coupled, fsem, csem, bsem):
    ni, width = coupling.shape
    nblk = lax.axis_size("grp")
    blk = width // nblk
    steps = ni // TILE
    rows = [pl.ds(i * TILE, TILE) for i in range(steps)]
    loads = []
    for i in range(steps):
        ccopy = pltpu.make_async_copy(coupling.at[rows[i]], cbuf.at[rows[i]], csem.at[i])
        span = pl.ds(0, (i + 1) * TILE)
        fcopy = pltpu.make_async_copy(factor.at[rows[i], span], fbuf.at[rows[i], span], fsem.at[i])
        ccopy.start()
        fcopy.start()
        loads.append((ccopy, fcopy))
    bcopy = pltpu.make_async_copy(block, bbuf, bsem)
    bcopy.start()
    for i in range(steps):
        for copy in loads[i]:
            copy.wait()
        span = (i + 1) * TILE
        part = jnp.dot(
            fbuf[rows[i], 0:span], cbuf[0:span, :], preferred_element_type=jnp.float32
        )
        coupled[rows[i], :] = part.astype(jnp.bfloat16)
    gram = lax.dot_general(
        coupled[...], coupled[...], (((0,), (0,)), ((), ())), preferred_element_type=jnp.float32
    )
    bcopy.wait()
    member = lax.axis_index("grp")
    count = live[0]
    for a in range(nblk):
        row = pl.multiple_of(lax.rem(a - member + nblk, nblk) * blk, blk)
        for b in range(nblk):
            col = pl.multiple_of(lax.rem(member - b + nblk, nblk) * blk, blk)
            cut = (slice(a * blk, (a + 1) * blk), slice(b * blk, (b + 1) * blk))
            scale = jnp.where(max(a, b) < count, 0.5, 0.0).astype(jnp.float32)
            value = (bbuf[cut] - gram[cut]) * scale
            top = value.astype(jnp.bfloat16)
            high[pl.ds(row, blk), pl.ds(col, blk)] = top
            low[pl.ds(row, blk), pl.ds(col, blk)] = (value - top.astype(jnp.float32)).astype(
                jnp.bfloat16
            )


def first_kernel(ids, high, low, own, near, far, *terms):
    nblk = len(terms)
    blk = own.shape[0] // nblk
    member = lax.axis_index("grp")
    even = lax.rem(member, 2) == 0
    picked = []
    for r in range(nblk):
        b = lax.rem(member - r + nblk, nblk)
        span = pl.ds(pl.multiple_of(b * blk, blk), blk)
        dest = offset_of(ids, b)
        use_near = jnp.logical_or(
            jnp.logical_and(dest == -1, even), jnp.logical_and(dest == 1, jnp.logical_not(even))
        )
        other = jnp.where(use_near, near[span, :], far[span, :])
        picked.append(jnp.where(dest == 0, own[span, :], other))
    vector = jnp.concatenate(picked, axis=0).astype(jnp.bfloat16)
    product = jnp.dot(high[...], vector, preferred_element_type=jnp.float32)
    product = product + jnp.dot(low[...], vector, preferred_element_type=jnp.float32)
    for r in range(nblk):
        terms[r][0:blk, :] = product[r * blk : (r + 1) * blk, :]
        dest = offset_of(ids, lax.rem(member + r, nblk))
        terms[r][blk : blk + TAIL, :] = jnp.full(
            (TAIL, own.shape[1]), dest.astype(jnp.float32), jnp.float32
        )


def apply_kernel(high, low, *refs):
    nblk = len(refs) // 2
    blk = refs[0].shape[0]
    vector = jnp.concatenate([ref[...] for ref in refs[:nblk]], axis=0)
    top = vector.astype(jnp.bfloat16)
    rest = (vector - top.astype(jnp.float32)).astype(jnp.bfloat16)
    product = jnp.dot(high[...], top, preferred_element_type=jnp.float32)
    product = product + jnp.dot(high[...], rest, preferred_element_type=jnp.float32)
    product = product + jnp.dot(low[...], top, preferred_element_type=jnp.float32)
    for r in range(nblk):
        refs[nblk + r][...] = product[r * blk : (r + 1) * blk, :]


def local(
    interior_factor, interface_coupling, interface_block, sample_panel, index_map, block_count
):
    factor = interior_factor[0]
    coupling = interface_coupling[0]
    block = interface_block[0]
    nblk = index_map.shape[1]
    ni, width = coupling.shape
    blk = width // nblk
    samples = sample_panel.shape[1]
    cycles = lax.axis_size("sub")
    groups = lax.axis_size("grp")
    assert nblk == groups
    smem = pl.BlockSpec(memory_space=pltpu.SMEM)
    anywhere = pl.BlockSpec(memory_space=pltpu.HBM)
    vmem = pl.BlockSpec(memory_space=pltpu.VMEM)

    small = pltpu.CompilerParams(vmem_limit_bytes=8 * 1024 * 1024)
    own = sample_panel.astype(jnp.float32)
    route = []
    for o in range(cycles):
        for g in range(groups):
            step = 1 if g % 2 == 0 else -1
            route.append((o * groups + g, ((o + step) % cycles) * groups + g))
    near = lax.ppermute(own, ("sub", "grp"), route)

    steps = ni // TILE
    half = jax.ShapeDtypeStruct((width, width), jnp.bfloat16)
    high, low = pl.pallas_call(
        schur_kernel,
        out_shape=(half, half),
        in_specs=[smem, anywhere, anywhere, anywhere],
        out_specs=(vmem, vmem),
        scratch_shapes=[
            pltpu.VMEM((ni, ni), jnp.bfloat16),
            pltpu.VMEM((ni, width), jnp.bfloat16),
            pltpu.VMEM((width, width), jnp.float32),
            pltpu.VMEM((ni, width), jnp.bfloat16),
            pltpu.SemaphoreType.DMA((steps,)),
            pltpu.SemaphoreType.DMA((steps,)),
            pltpu.SemaphoreType.DMA,
        ],
        cost_estimate=pl.CostEstimate(
            flops=ni * ni * width + 2 * ni * width * width,
            bytes_accessed=ni * ni + 2 * ni * width + 4 * width * width,
            transcendentals=0,
        ),
        compiler_params=pltpu.CompilerParams(vmem_limit_bytes=52 * 1024 * 1024),
        name="schur",
    )(block_count, factor, coupling, block)

    near, high = lax.optimization_barrier((near, high))
    far = lax.ppermute(near, "grp", [(g, g ^ 1) for g in range(groups)])
    tall = jax.ShapeDtypeStruct((blk + TAIL, samples), jnp.float32)
    short = jax.ShapeDtypeStruct((blk, samples), jnp.float32)
    terms = pl.pallas_call(
        first_kernel,
        out_shape=(tall,) * nblk,
        in_specs=[smem] + [vmem] * 5,
        out_specs=(vmem,) * nblk,
        compiler_params=small,
        name="first",
    )(index_map, high, low, own, near, far)

    owners = None
    even = lax.axis_index("grp") % 2 == 0
    for step in range(POWER):
        if step > 0:
            terms = pl.pallas_call(
                apply_kernel,
                out_shape=(short,) * nblk,
                in_specs=[vmem] * (2 + nblk),
                out_specs=(vmem,) * nblk,
                compiler_params=small,
                name="apply",
            )(high, low, *picked)
        got = [terms[0]] + [grp_shift(terms[r], r) for r in range(1, groups)]
        if step == 0:
            owners = [g[blk : blk + 1, :] for g in got]
            got = [g[:blk] for g in got]
        zero = jnp.zeros((blk, samples), jnp.float32)
        sums = {}
        for d in (-1, 0, 1):
            sums[d] = sum(jnp.where(owners[r] == d, got[r], zero) for r in range(groups))
        if step + 1 < POWER:
            behind, ahead = cross_shift(
                jnp.concatenate([sums[0], sums[1]]), jnp.concatenate([sums[0], sums[-1]]), 1, even
            )
            behind2 = sub_shift(sums[1], 2)
            ahead2 = sub_shift(sums[-1], -2)
            here = sums[0] + behind[blk:] + ahead[blk:]
            after = ahead[:blk] + sums[1] + ahead2
            before = behind[:blk] + sums[-1] + behind2
            picked = []
            for r in range(groups):
                owner = owners[(groups - r) % groups]
                chosen = jnp.where(owner == 0, here, jnp.where(owner == 1, after, before))
                picked.append(chosen if r == 0 else grp_shift(chosen, r))
    return sums[0] + sub_shift(sums[1], 1) + sub_shift(sums[-1], -1)


def solution(mesh):
    return jax.shard_map(
        local,
        mesh=mesh,
        in_specs=(
            P(("sub", "grp"), None, None),
            P(("sub", "grp"), None, None),
            P(("sub", "grp"), None, None),
            P("sub", None),
            P(("sub", "grp"), None),
            P(("sub", "grp")),
        ),
        out_specs=P(("sub", "grp"), None),
        check_vma=False,
    )
```
